32 devices in a mesh: ang: 16 (over z, x, core), strip: 2 (over y).
Axes of the slice: x: 2, y: 2, z: 4, core: 2. Of those that a mesh axis runs over, the one named last changes fastest.
Arguments:
- measured: float32 [16, 16, 128, 128], P('ang', 'strip'), may hold values from 0.05 to 4
- positions: int32 [16, 16], P('ang', 'strip'), may hold values from 0 to 384
- probe_field: float32 [2, 128, 128], replicated, may hold values from -6 to 6
- object_field: float32 [16, 512, 2, 128], P('ang', 'strip'), may hold values from -6 to 6
- dual_field: float32 [16, 512, 2, 128], P('ang', 'strip'), may hold values from -6 to 6
- volume: float32 [8192, 2, 128], P(('ang', 'strip')), may hold values from -6 to 6
- radon_tiles: bfloat16 [32, 16, 2, 32, 256], P(('ang', 'strip')), may hold values from -0.1875 to 0.1875
- tile_range: int32 [16, 16, 2, 1], P('ang', None, 'strip'), may hold values from 0 to 14
Outputs:
- object_next: float32 [16, 512, 2, 128], P('ang', 'strip')
- dual_next: float32 [16, 512, 2, 128], P('ang', 'strip')
- volume_next: float32 [8192, 2, 128], P(('ang', 'strip'))
The draws below stay inside these ranges and needn't reach their ends.
Inputs may be any that keep to these rules, and one draw needn't show every extreme that they name: `positions`: a frame covers 128 detector columns from its position. A pixel tile meets ray tiles tile_range to tile_range + 1 at that angle.
All inputs are finite; a program needn't handle non-finite values.
Results may differ from the reference program's by a relative error of at most 0.0027.
Values may be sent and summed in bfloat16 or wider, within the bound.
A program may use at most 64 MiB of HBM per device.

```python
import math
import jax
import jax.numpy as jnp
from jax import lax

PROBE = 128
NZ = 128
NDET = 512
RAYS = 32
TILE = 256
HITS = 2
PT_DEV = 1
NANG = 16
FR = 16
NPT = 32
NPIX = 8192
NR = 16
N_ANG = 16
N_STRIP = 2


def with_ends(array, own_key, least, top_value):
    index_at = [jax.random.randint(jax.random.fold_in(own_key, axis), (), 0, length) for axis, length in enumerate(array.shape)]
    longest = array.shape.index(max(array.shape))
    next_to = index_at[:longest] + [(index_at[longest] + 1) % array.shape[longest]] + index_at[longest + 1:]
    return array.at[tuple(index_at)].set(least).at[tuple(next_to)].set(top_value)


def steps_of(stream_key, shape, split, low, largest):
    factor_of = 1.0
    for axis_at, parts in split:
        heights = jax.random.uniform(jax.random.fold_in(jax.random.fold_in(stream_key, 6), axis_at), (parts,), jnp.float32, low / len(split), largest / len(split))
        factor_of = factor_of * jnp.repeat(jnp.exp(heights), shape[axis_at] // parts).reshape((-1,) + (1,) * (len(shape) - 1 - axis_at))
    return factor_of


def noise(key, shape, scale, most, cuts=(), kind=jnp.bfloat16):
    gain = steps_of(key, shape, cuts, -0.22, 0.18) if cuts else 1.0
    result = jax.random.normal(key, shape, jnp.float32) * scale * gain
    return jnp.minimum(jnp.maximum(result, -most), most).astype(kind)


def setup_inputs(seed: int = 0) -> dict:
    key_of = jax.random.split(jax.random.key(seed), 9)
    return {
        "measured": jnp.clip(jnp.exp(math.log(4.0) - 4.3820266 * jax.random.uniform(key_of[0], (NANG, FR, PROBE, PROBE), jnp.float32) ** steps_of(key_of[0], (NANG, FR, PROBE, PROBE), ((0, 16), (1, 2)), -0.2, 0.2)), 0.05, 4.0),
        "positions": with_ends(jax.random.randint(key_of[1], (NANG, FR), 0, NDET - PROBE + 1), jax.random.fold_in(key_of[1], 1), 0, NDET - PROBE).astype(jnp.int32),
        "probe_field": noise(key_of[2], (2, PROBE, PROBE), 1.0, 6.0, (), jnp.float32),
        "object_field": noise(key_of[3], (NANG, NDET, 2, NZ), 1.0, 6.0, ((0, 16), (1, 2)), jnp.float32),
        "dual_field": noise(key_of[4], (NANG, NDET, 2, NZ), 1.0, 6.0, ((0, 16), (1, 2)), jnp.float32),
        "volume": noise(key_of[5], (NPIX, 2, NZ), 1.0, 6.0, ((0, 32),), jnp.float32),
        "radon_tiles": noise(key_of[6], (NPT, NANG, HITS, RAYS, TILE), (HITS * NPT * TILE // NR) ** -0.5, 0.1875, ((0, 32),)),
        "tile_range": with_ends(jax.random.randint(key_of[7], (NANG, N_ANG, N_STRIP, PT_DEV), 0, NR - HITS + 1), jax.random.fold_in(key_of[7], 1), 0, NR - HITS).astype(jnp.int32),
    }


penalty = 1.0
object_step = 0.1
volume_step = 1.0
precise = lax.Precision.HIGHEST

def dft_tables(length):
    indices = jnp.arange(length, dtype=jnp.int32)
    phases = indices[:, None] * indices[None, :] % length
    angles = phases.astype(jnp.float32) * (2.0 * math.pi / length)
    scaling = 1.0 / math.sqrt(length)
    return (jnp.cos(angles) * scaling, jnp.sin(angles) * scaling)

def transform(real_part, imag_part, cosine_table, sine_table, handed):
    left_re = jnp.einsum('kc,fcr->fkr', cosine_table, real_part, precision=precise) + handed * jnp.einsum('kc,fcr->fkr', sine_table, imag_part, precision=precise)
    left_im = jnp.einsum('kc,fcr->fkr', cosine_table, imag_part, precision=precise) - handed * jnp.einsum('kc,fcr->fkr', sine_table, real_part, precision=precise)
    out_re = jnp.einsum('fkr,rl->fkl', left_re, cosine_table, precision=precise) + handed * jnp.einsum('fkr,rl->fkl', left_im, sine_table, precision=precise)
    out_im = jnp.einsum('fkr,rl->fkl', left_im, cosine_table, precision=precise) - handed * jnp.einsum('fkr,rl->fkl', left_re, sine_table, precision=precise)
    return (out_re, out_im)

def intersection_gradient(intensity, starts, field, probe_field, cosine_table, sine_table):
    window = probe_field.shape[1]

    def cutout(start):
        return lax.dynamic_slice_in_dim(field, start, window, 0)
    patches = jax.vmap(cutout)(starts)
    object_re = patches[:, :, 0, :]
    object_im = patches[:, :, 1, :]
    probe_re = probe_field[0]
    probe_im = probe_field[1]
    wave_re = probe_re * object_re - probe_im * object_im
    wave_im = probe_re * object_im + probe_im * object_re
    far_re, far_im = transform(wave_re, wave_im, cosine_table, sine_table, 1.0)
    modulus = jnp.sqrt(far_re * far_re + far_im * far_im)
    shrink = 1.0 - jnp.sqrt(intensity) / jnp.maximum(modulus, 1.0)
    back_re, back_im = transform(far_re * shrink, far_im * shrink, cosine_table, sine_table, -1.0)
    grad_re = probe_re * back_re + probe_im * back_im
    grad_im = probe_re * back_im - probe_im * back_re
    frame_grads = jnp.stack([grad_re, grad_im], axis=2)

    def deposit(index, total):
        piece = lax.dynamic_slice_in_dim(total, starts[index], window, 0)
        return lax.dynamic_update_slice_in_dim(total, piece + frame_grads[index], starts[index], 0)
    return lax.fori_loop(0, starts.shape[0], deposit, jnp.zeros(field.shape, jnp.float32))

def reference(measured, positions, probe_field, object_field, dual_field, volume, radon_tiles, tile_range):
    cosine_table, sine_table = dft_tables(PROBE)

    def ptycho_angle(inputs):
        intensity, starts, field = inputs
        return intersection_gradient(intensity, starts, field, probe_field, cosine_table, sine_table)
    intersection = lax.map(ptycho_angle, (measured, positions, object_field))
    volume_half = lax.optimization_barrier(volume.astype(jnp.bfloat16)).astype(jnp.float32).reshape(NPT, TILE, 2 * NZ)
    ranges = tile_range.reshape(NANG, NPT)
    hit_offsets = jnp.arange(HITS, dtype=jnp.int32)
    range_ids = jnp.arange(NR, dtype=jnp.int32)

    def tiles_at(angle_index):
        return lax.dynamic_index_in_dim(radon_tiles, angle_index, 1, keepdims=False).astype(jnp.float32)

    def targets_at(angle_index):
        return (ranges[angle_index][:, None] + hit_offsets[None, :]).reshape(NPT * HITS)

    def project_angle(angle_index):
        partials = jnp.einsum('phrt,ptc->phrc', tiles_at(angle_index), volume_half, precision=precise)
        selector = (range_ids[:, None] == targets_at(angle_index)[None, :]).astype(jnp.float32)
        dense_rows = jnp.dot(selector, partials.reshape(NPT * HITS, RAYS * 2 * NZ), precision=precise)
        return dense_rows.reshape(NDET, 2, NZ)
    projection = lax.map(project_angle, jnp.arange(NANG, dtype=jnp.int32))
    object_next = object_field - object_step * (intersection + dual_field + penalty * (object_field - projection))
    dual_next = dual_field + penalty * (object_next - projection)
    residual = lax.optimization_barrier((penalty * (projection - object_next) - dual_field).astype(jnp.bfloat16)).astype(jnp.float32)

    def back_angle(total, angle_index):
        selector = (targets_at(angle_index)[:, None] == range_ids[None, :]).astype(jnp.float32)
        rows = residual[angle_index].reshape(NR, RAYS * 2 * NZ)
        picked = jnp.dot(selector, rows, precision=precise).reshape(NPT, HITS, RAYS, 2 * NZ)
        return (total + jnp.einsum('phrt,phrc->ptc', tiles_at(angle_index), picked, precision=precise), None)
    gradient, unused = lax.scan(back_angle, jnp.zeros((NPT, TILE, 2 * NZ), jnp.float32), jnp.arange(NANG, dtype=jnp.int32))
    volume_next = volume - volume_step * gradient.reshape(NPIX, 2, NZ)
    return (object_next, dual_next, volume_next)
```

```python
import functools
import math

import jax
import jax.numpy as jnp
import numpy as np
from jax import lax
from jax.experimental import pallas as pl
from jax.experimental.pallas import tpu as pltpu
from jax.sharding import PartitionSpec as P

RAYS = 32

penalty = 1.0
object_step = 0.1
volume_step = 1.0
MESH = pl.DeviceIdType.MESH


def dft_tables(length):
    indices = np.arange(length, dtype=np.int64)
    angles = (indices[:, None] * indices[None, :] % length) * (2.0 * math.pi / length)
    scaling = 1.0 / math.sqrt(length)
    parts = []
    for table in (np.cos(angles) * scaling, np.sin(angles) * scaling):
        table = table.astype(np.float32)
        high = table.astype(jnp.bfloat16)
        parts += [high, (table - high.astype(np.float32)).astype(jnp.bfloat16)]
    return np.stack(parts)


def split(value):
    high = value.astype(jnp.bfloat16)
    return high, (value - high.astype(jnp.float32)).astype(jnp.bfloat16)


def dot(left, right):
    return jnp.dot(left, right, preferred_element_type=jnp.float32)


def dot3(left, right):
    return dot(left[0], right[0]) + (dot(left[0], right[1]) + dot(left[1], right[0]))


def beside(left, right):
    return jnp.concatenate([left, right], axis=1)


def above(top, low):
    return jnp.concatenate([top, low], axis=0)


def swap_blocks(value):
    half = value.shape[1] // 2
    return above(
        beside(value[:half, :half], value[half:, :half]),
        beside(value[:half, half:], value[half:, half:]),
    )


def both_parts(ref, columns):
    return beside(ref[pl.ds(0, columns, stride=2), :], ref[pl.ds(1, columns, stride=2), :])


def put_parts(ref, value):
    columns, half = value.shape[0], value.shape[1] // 2
    ref[pl.ds(0, columns, stride=2), :] = value[:, :half]
    ref[pl.ds(1, columns, stride=2), :] = value[:, half:]


def window(start, count, rows):
    first = lax.broadcasted_iota(jnp.int32, (count, rows), 0) + start
    return one_where(first == lax.broadcasted_iota(jnp.int32, (count, rows), 1))


def one_where(mask):
    return jnp.where(mask, 1.0, 0.0).astype(jnp.bfloat16)


def one_hot(rows, starts, count, width, scale):
    lanes = lax.broadcasted_iota(jnp.int32, (1, count * width), 1)
    block = lanes // width
    target = lanes % width
    for k in range(count):
        target = target + jnp.where(block == k, starts[k] * scale, 0)
    row = lax.broadcasted_iota(jnp.int32, (rows, count * width), 0)
    return one_where(row == target)


def kernel(
    angles, strips, order,
    positions, ranges, measured, probe, field, dual, volume, radon, tables,
    object_next, dual_next, volume_next,
    ray_out, ray_in, pick_out, pick_in, field_out, field_in, grad_out, grad_in,
    dense_out, dense_in, rows_half, whole_field, grads, total_grad, total_rays, gathered_radon, picker,
    ray_send, ray_recv, pick_send, pick_recv, strip_send, strip_recv,
):
    me, strip = lax.axis_index("ang"), lax.axis_index("strip")
    columns = field.shape[0] // 2
    detector = strips * columns
    frames, side = measured.shape[0], measured.shape[1]
    hit_rows = ray_out.shape[1]
    ang_peers = [lax.rem(me + offset, angles) for offset in order]
    strip_peers = [lax.rem(strip + offset, strips) for offset in range(1, strips)]
    own = pl.ds(pl.multiple_of(strip * columns, columns), columns)

    barrier = pltpu.get_barrier_semaphore()
    for peer in ang_peers:
        pl.semaphore_signal(barrier, inc=1, device_id=(peer, strip), device_id_type=MESH)
    for peer in strip_peers:
        pl.semaphore_signal(barrier, inc=1, device_id=(me, peer), device_id_type=MESH)

    own_field = both_parts(field, columns)
    field_out[...] = own_field.astype(jnp.bfloat16)
    volume_half = both_parts(volume, volume.shape[0] // 2).astype(jnp.bfloat16)
    sums = dot(radon[...], volume_half).astype(jnp.bfloat16)
    ray_out[...] = sums.reshape(ray_out.shape)
    pl.semaphore_wait(barrier, len(ang_peers) + len(strip_peers))

    def strip_copy(source, target, stage, slot, peer):
        return pltpu.make_async_remote_copy(
            src_ref=source, dst_ref=target,
            send_sem=strip_send.at[stage, peer], recv_sem=strip_recv.at[stage, slot],
            device_id=(me, peer), device_id_type=MESH,
        )

    def ang_copy(source, target, send, recv, slot, peer):
        return pltpu.make_async_remote_copy(
            src_ref=source, dst_ref=target, send_sem=send.at[peer], recv_sem=recv.at[slot],
            device_id=(peer, strip), device_id_type=MESH,
        )

    started = []

    def start(copy):
        copy.start()
        started.append(copy)

    for peer in strip_peers:
        start(strip_copy(field_out, field_in.at[strip], 0, strip, peer))
    for peer in ang_peers:
        start(ang_copy(ray_out.at[peer], ray_in.at[me], ray_send, ray_recv, me, peer))
    ray_in[me] = ray_out[me]

    gathered_radon[...] = radon[...].T
    cos_high, cos_low, sin_high, sin_low = (tables[k] for k in range(4))
    turn = tuple(
        above(beside(c, -s), beside(s, c)) for c, s in ((cos_high, sin_high), (cos_low, sin_low))
    )
    back_turn = tuple(
        above(beside(c, s), beside(-s, c)) for c, s in ((cos_high, sin_high), (cos_low, sin_low))
    )
    probe_re, probe_im = probe[0], probe[1]
    whole_field[own, :] = own_field
    for peer in strip_peers:
        strip_copy(field_out, field_in.at[peer], 0, peer, peer).wait_recv()
        rows = pl.ds(pl.multiple_of(peer * columns, columns), columns)
        whole_field[rows, :] = field_in[peer].astype(jnp.float32)

    field_high, field_low = split(whole_field[...])
    for pair in range(0, frames, 2):
        waves = []
        for j in (pair, pair + 1):
            cut = window(positions[j], side, detector)
            patch = dot(cut, field_high) + dot(cut, field_low)
            re, im = patch[:, :side], patch[:, side:]
            waves.append(beside(probe_re * re - probe_im * im, probe_re * im + probe_im * re))
        right = dot3(split(above(*waves)), turn)
        far = dot3(back_turn, split(swap_blocks(right)))
        far_re, far_im = far[:side], far[side:]
        modulus = jnp.sqrt(far_re * far_re + far_im * far_im)
        intensity = beside(measured[pair], measured[pair + 1])
        shrink = 1.0 - jnp.sqrt(intensity) / jnp.maximum(modulus, 1.0)
        left = dot3(turn, split(above(far_re * shrink, far_im * shrink)))
        back = dot3(split(swap_blocks(left)), back_turn)
        for k in range(2):
            part = back[k * side:(k + 1) * side]
            re, im = part[:, :side], part[:, side:]
            grads[(pair + k) * side:(pair + k + 1) * side, :] = beside(
                probe_re * re + probe_im * im, probe_re * im - probe_im * re
            )
    deposit = one_hot(detector, [positions[j] for j in range(frames)], frames, side, 1)
    high, low = split(grads[...])
    total_grad[...] = dot(deposit, high) + dot(deposit, low)
    for k in range(strips):
        grad_out[k] = total_grad[k * columns:(k + 1) * columns, :].astype(jnp.bfloat16)
    for peer in strip_peers:
        start(strip_copy(grad_out.at[peer], grad_in.at[strip], 1, strip, peer))

    selector = one_hot(
        detector, [ranges[k] for k in range(angles)], angles, hit_rows, RAYS
    )
    for k in range(angles):
        picker[k] = window(ranges[k] * RAYS, hit_rows, detector)
    for peer in ang_peers:
        ang_copy(ray_out.at[peer], ray_in.at[peer], ray_send, ray_recv, peer, peer).wait_recv()
    total_rays[...] = dot(selector, ray_in[...].reshape(angles * hit_rows, ray_in.shape[2]))
    for k in range(strips):
        dense_out[k] = total_rays[k * columns:(k + 1) * columns, :].astype(jnp.bfloat16)
    for peer in strip_peers:
        start(strip_copy(dense_out.at[peer], dense_in.at[strip], 2, strip, peer))

    intersection = total_grad[own, :]
    for peer in strip_peers:
        strip_copy(grad_out.at[peer], grad_in.at[peer], 1, peer, peer).wait_recv()
        intersection = intersection + grad_in[peer].astype(jnp.float32)
    projection = total_rays[own, :]
    for peer in strip_peers:
        strip_copy(dense_out.at[peer], dense_in.at[peer], 2, peer, peer).wait_recv()
        projection = projection + dense_in[peer].astype(jnp.float32)
    own_dual = both_parts(dual, columns)
    own_field = whole_field[own, :]
    updated = own_field - object_step * (
        intersection + own_dual + penalty * (own_field - projection)
    )
    residual = penalty * (projection - updated) - own_dual
    rows_half[own, :] = residual.astype(jnp.bfloat16)
    for peer in strip_peers:
        start(strip_copy(rows_half.at[own], rows_half.at[own], 3, strip, peer))
    put_parts(object_next, updated)
    put_parts(dual_next, own_dual + penalty * (updated - projection))
    for peer in strip_peers:
        rows = pl.ds(pl.multiple_of(peer * columns, columns), columns)
        strip_copy(rows_half.at[rows], rows_half.at[rows], 3, peer, peer).wait_recv()

    rows = rows_half[...]
    for peer in ang_peers:
        pick_out[peer] = dot(picker[peer], rows).astype(jnp.bfloat16)
        start(ang_copy(pick_out.at[peer], pick_in.at[me], pick_send, pick_recv, me, peer))
    pick_in[me] = dot(picker[me], rows).astype(jnp.bfloat16)
    own_volume = both_parts(volume, volume.shape[0] // 2)
    for peer in ang_peers:
        ang_copy(pick_out.at[peer], pick_in.at[peer], pick_send, pick_recv, peer, peer).wait_recv()
    gradient = dot(
        gathered_radon[...], pick_in[...].reshape(angles * hit_rows, pick_in.shape[2])
    )
    put_parts(volume_next, own_volume - volume_step * gradient)
    for copy in started:
        copy.wait_send()


def body(
    measured, positions, probe_field, object_field, dual_field, volume, radon_tiles, tile_range
):
    angles, strips = lax.axis_size("ang"), lax.axis_size("strip")
    order = sorted(range(1, angles), key=lambda offset: abs(offset - angles // 2))
    frames, side = measured.shape[1], measured.shape[2]
    columns, width = object_field.shape[1], object_field.shape[2] * object_field.shape[3]
    hit_rows = radon_tiles.shape[2] * radon_tiles.shape[3]
    pixels = radon_tiles.shape[4]
    slices = object_field.shape[3]
    vmem = pl.BlockSpec(memory_space=pltpu.VMEM)
    smem = pl.BlockSpec(memory_space=pltpu.SMEM)
    half = jnp.bfloat16
    outs = pl.pallas_call(
        functools.partial(kernel, angles, strips, order),
        out_shape=(
            jax.ShapeDtypeStruct((2 * columns, slices), jnp.float32),
            jax.ShapeDtypeStruct((2 * columns, slices), jnp.float32),
            jax.ShapeDtypeStruct((2 * pixels, slices), jnp.float32),
        ),
        in_specs=[smem, smem] + [vmem] * 7,
        out_specs=(vmem, vmem, vmem),
        scratch_shapes=[
            pltpu.VMEM((angles, hit_rows, width), half),
            pltpu.VMEM((angles, hit_rows, width), half),
            pltpu.VMEM((angles, hit_rows, width), half),
            pltpu.VMEM((angles, hit_rows, width), half),
            pltpu.VMEM((columns, width), half),
            pltpu.VMEM((strips, columns, width), half),
            pltpu.VMEM((strips, columns, width), half),
            pltpu.VMEM((strips, columns, width), half),
            pltpu.VMEM((strips, columns, width), half),
            pltpu.VMEM((strips, columns, width), half),
            pltpu.VMEM((strips * columns, width), half),
            pltpu.VMEM((strips * columns, width), jnp.float32),
            pltpu.VMEM((frames * side, width), jnp.float32),
            pltpu.VMEM((strips * columns, width), jnp.float32),
            pltpu.VMEM((strips * columns, width), jnp.float32),
            pltpu.VMEM((pixels, angles * hit_rows), half),
            pltpu.VMEM((angles, hit_rows, strips * columns), half),
            pltpu.SemaphoreType.DMA((angles,)),
            pltpu.SemaphoreType.DMA((angles,)),
            pltpu.SemaphoreType.DMA((angles,)),
            pltpu.SemaphoreType.DMA((angles,)),
            pltpu.SemaphoreType.DMA((4, strips)),
            pltpu.SemaphoreType.DMA((4, strips)),
        ],
        compiler_params=pltpu.CompilerParams(
            collective_id=0, has_side_effects=True, vmem_limit_bytes=48 * 1024 * 1024
        ),
    )(
        positions.reshape(frames),
        tile_range.reshape(angles),
        measured[0],
        probe_field,
        object_field.reshape(2 * columns, slices),
        dual_field.reshape(2 * columns, slices),
        volume.reshape(2 * pixels, slices),
        radon_tiles.reshape(angles * hit_rows, pixels),
        jnp.asarray(dft_tables(side)),
    )
    return (
        outs[0].reshape(object_field.shape),
        outs[1].reshape(dual_field.shape),
        outs[2].reshape(volume.shape),
    )


def solution(mesh):
    return jax.shard_map(
        body,
        mesh=mesh,
        in_specs=(
            P("ang", "strip", None, None),
            P("ang", "strip"),
            P(),
            P("ang", "strip", None, None),
            P("ang", "strip", None, None),
            P(("ang", "strip"), None, None),
            P(("ang", "strip"), None, None, None, None),
            P("ang", None, "strip", None),
        ),
        out_specs=(
            P("ang", "strip", None, None),
            P("ang", "strip", None, None),
            P(("ang", "strip"), None, None),
        ),
        check_vma=False,
    )
```

```python
import functools
import math

import jax
import jax.numpy as jnp
import numpy as np
from jax import lax
from jax.experimental import pallas as pl
from jax.experimental.pallas import tpu as pltpu
from jax.sharding import PartitionSpec as P

RAYS = 32
VMEM_BYTES = 67043328

penalty = 1.0
object_step = 0.1
volume_step = 1.0
MESH = pl.DeviceIdType.MESH


def dft_tables(length):
    indices = np.arange(length, dtype=np.int64)
    angles = (indices[:, None] * indices[None, :] % length) * (2.0 * math.pi / length)
    scaling = 1.0 / math.sqrt(length)
    parts = []
    for table in (np.cos(angles) * scaling, np.sin(angles) * scaling):
        table = table.astype(np.float32)
        high = table.astype(jnp.bfloat16)
        parts += [high, (table - high.astype(np.float32)).astype(jnp.bfloat16)]
    return np.stack(parts)


def split(value):
    high = value.astype(jnp.bfloat16)
    return high, (value - high.astype(jnp.float32)).astype(jnp.bfloat16)


def dot(left, right):
    return jnp.dot(left, right, preferred_element_type=jnp.float32)


def dot3(left, right):
    return dot(left[0], right[0]) + (dot(left[0], right[1]) + dot(left[1], right[0]))


def beside(left, right):
    return jnp.concatenate([left, right], axis=1)


def above(top, low):
    return jnp.concatenate([top, low], axis=0)


def swap_blocks(value):
    half = value.shape[1] // 2
    return above(
        beside(value[:half, :half], value[half:, :half]),
        beside(value[:half, half:], value[half:, half:]),
    )


def both_parts(ref, columns):
    return beside(ref[pl.ds(0, columns, stride=2), :], ref[pl.ds(1, columns, stride=2), :])


def put_parts(ref, value):
    columns, half = value.shape[0], value.shape[1] // 2
    ref[pl.ds(0, columns, stride=2), :] = value[:, :half]
    ref[pl.ds(1, columns, stride=2), :] = value[:, half:]


def window(start, count, rows):
    first = lax.broadcasted_iota(jnp.int32, (count, rows), 0) + start
    return one_where(first == lax.broadcasted_iota(jnp.int32, (count, rows), 1))


def one_where(mask):
    return jnp.where(mask, 1.0, 0.0).astype(jnp.bfloat16)


def one_hot(rows, starts, count, width, scale):
    lanes = lax.broadcasted_iota(jnp.int32, (1, count * width), 1)
    block = lanes // width
    target = lanes % width
    for k in range(count):
        target = target + jnp.where(block == k, starts[k] * scale, 0)
    row = lax.broadcasted_iota(jnp.int32, (rows, count * width), 0)
    return one_where(row == target)


def xor(left, right, bound):
    result, bit = 0, 1
    while bit < bound:
        result = result + ((left // bit) + (right // bit)) % 2 * bit
        bit *= 2
    return result


def kernel(
    angles, strips,
    positions, ranges, measured_hbm, probe_hbm, field_hbm, dual_hbm, volume_hbm, radon_hbm,
    tables_hbm,
    object_next, dual_next, volume_next,
    measured, probe, field, dual, volume, radon, tables,
    ray_out, ray_in, pick_out, pick_in, field_out, field_in, grad_out, grad_in,
    dense_out, dense_in, rows_half, whole_field, grads, total_grad, total_rays, turned_radon,
    picker, selector,
    load_sem, ray_send, ray_recv, pick_send, pick_recv, strip_send, strip_recv,
):
    loads = {}
    for k, (name, source, target) in enumerate((
        ("volume", volume_hbm, volume), ("radon", radon_hbm, radon), ("field", field_hbm, field),
        ("tables", tables_hbm, tables), ("probe", probe_hbm, probe),
        ("measured", measured_hbm, measured), ("dual", dual_hbm, dual),
    )):
        loads[name] = pltpu.make_async_copy(source, target, load_sem.at[k])
        loads[name].start()
    me, strip = lax.axis_index("ang"), lax.axis_index("strip")
    columns = field.shape[0] // 2
    detector = strips * columns
    frames, side = measured.shape[0], measured.shape[1]
    slices = field.shape[1]
    chunks, hit_rows = ray_out.shape[0], ray_out.shape[2]
    if angles & (angles - 1):
        ang_peers = [lax.rem(me + offset, angles) for offset in range(1, angles)]
    else:
        ang_peers = [xor(me, offset, angles) for offset in range(angles - 1, 0, -1)]
    strip_peers = [lax.rem(strip + offset, strips) for offset in range(1, strips)]

    def rows_of(owner):
        return pl.ds(pl.multiple_of(owner * columns, columns), columns)

    barrier = pltpu.get_barrier_semaphore()
    for peer in ang_peers:
        pl.semaphore_signal(barrier, inc=1, device_id=(peer, strip), device_id_type=MESH)
    for peer in strip_peers:
        pl.semaphore_signal(barrier, inc=1, device_id=(me, peer), device_id_type=MESH)

    loads["volume"].wait()
    loads["radon"].wait()
    pixels = volume.shape[0] // 2
    volume_half = both_parts(volume, pixels).astype(jnp.bfloat16)
    sums = dot(radon[...], volume_half).astype(jnp.bfloat16)
    for c in range(chunks):
        ray_out[c] = sums[:, c * slices:(c + 1) * slices].reshape(ray_out.shape[1:])
    loads["field"].wait()
    own_field = both_parts(field, columns)
    field_out[...] = own_field.astype(jnp.bfloat16)
    pl.semaphore_wait(barrier, len(ang_peers) + len(strip_peers))

    def strip_copy(source, target, stage, slot, peer):
        return pltpu.make_async_remote_copy(
            src_ref=source, dst_ref=target,
            send_sem=strip_send.at[stage, peer], recv_sem=strip_recv.at[stage, slot],
            device_id=(me, peer), device_id_type=MESH,
        )

    def ray_copy(c, slot, peer):
        return pltpu.make_async_remote_copy(
            src_ref=ray_out.at[c, peer], dst_ref=ray_in.at[c, slot],
            send_sem=ray_send.at[c, peer], recv_sem=ray_recv.at[c, slot],
            device_id=(peer, strip), device_id_type=MESH,
        )

    def pick_copy(c, slot, peer):
        return pltpu.make_async_remote_copy(
            src_ref=pick_out.at[c, peer], dst_ref=pick_in.at[c, slot],
            send_sem=pick_send.at[c, peer], recv_sem=pick_recv.at[c, slot],
            device_id=(peer, strip), device_id_type=MESH,
        )

    def grad_copy(c, slot, peer):
        return strip_copy(grad_out.at[c, peer], grad_in.at[c, slot], 1 + c, slot, peer)

    def dense_copy(c, slot, peer):
        return strip_copy(
            dense_out.at[c, peer], dense_in.at[c, slot], 1 + chunks + c, slot, peer
        )

    def residual_copy(c, owner, peer):
        part = rows_half.at[c, rows_of(owner), :]
        return strip_copy(part, part, 1 + 2 * chunks + c, owner, peer)

    started = []

    def start(copy):
        copy.start()
        started.append(copy)

    for peer in ang_peers:
        start(ray_copy(0, me, peer))
    for peer in strip_peers:
        start(strip_copy(field_out, field_in.at[strip], 0, strip, peer))
    for c in range(1, chunks):
        for peer in ang_peers:
            start(ray_copy(c, me, peer))

    for c in range(chunks):
        ray_in[c, me] = ray_out[c, me]
    selector[...] = one_hot(
        detector, [ranges[k] for k in range(angles)], angles, hit_rows, RAYS
    )
    for name in ("tables", "probe", "measured", "dual"):
        loads[name].wait()
    cos_high, cos_low, sin_high, sin_low = (tables[k] for k in range(4))
    turn = tuple(
        above(beside(c, -s), beside(s, c)) for c, s in ((cos_high, sin_high), (cos_low, sin_low))
    )
    back_turn = tuple(
        above(beside(c, s), beside(-s, c)) for c, s in ((cos_high, sin_high), (cos_low, sin_low))
    )
    probe_re, probe_im = probe[0], probe[1]
    whole_field[rows_of(strip), :] = own_field
    for peer in strip_peers:
        strip_copy(field_out, field_in.at[peer], 0, peer, peer).wait_recv()
        whole_field[rows_of(peer), :] = field_in[peer].astype(jnp.float32)
    field_high, field_low = split(whole_field[...])

    def frame_pair(pair):
        waves = []
        for j in (pair, pair + 1):
            cut = window(positions[j], side, detector)
            patch = dot(cut, field_high) + dot(cut, field_low)
            re, im = patch[:, :side], patch[:, side:]
            waves.append(beside(probe_re * re - probe_im * im, probe_re * im + probe_im * re))
        right = dot3(split(above(*waves)), turn)
        far = dot3(back_turn, split(swap_blocks(right)))
        far_re, far_im = far[:side], far[side:]
        modulus = jnp.sqrt(far_re * far_re + far_im * far_im)
        intensity = beside(measured[pair], measured[pair + 1])
        shrink = 1.0 - jnp.sqrt(intensity) / jnp.maximum(modulus, 1.0)
        left = dot3(turn, split(above(far_re * shrink, far_im * shrink)))
        back = dot3(split(swap_blocks(left)), back_turn)
        for k in range(2):
            part = back[k * side:(k + 1) * side]
            re, im = part[:, :side], part[:, side:]
            grads[(pair + k) * side:(pair + k + 1) * side, :] = beside(
                probe_re * re + probe_im * im, probe_re * im - probe_im * re
            )

    def sum_rays(c):
        for peer in ang_peers:
            ray_copy(c, peer, peer).wait_recv()
        total_rays[c] = dot(selector[...], ray_in[c].reshape(angles * hit_rows, slices))
        for k in range(strips):
            dense_out[c, k] = total_rays[c, k * columns:(k + 1) * columns].astype(jnp.bfloat16)
        for peer in strip_peers:
            start(dense_copy(c, strip, peer))

    middle = frames // 4 * 2
    for pair in range(0, middle, 2):
        frame_pair(pair)
    sum_rays(0)
    for pair in range(middle, frames, 2):
        frame_pair(pair)
    deposit = one_hot(detector, [positions[j] for j in range(frames)], frames, side, 1)
    high, low = split(grads[...])
    deposited = dot(deposit, high) + dot(deposit, low)
    for c in range(chunks):
        total_grad[c] = deposited[:, c * slices:(c + 1) * slices]
        for k in range(strips):
            grad_out[c, k] = total_grad[c, k * columns:(k + 1) * columns].astype(jnp.bfloat16)
        for peer in strip_peers:
            start(grad_copy(c, strip, peer))
    for c in range(1, chunks):
        sum_rays(c)
    for k in range(angles):
        picker[k] = window(ranges[k] * RAYS, hit_rows, detector)

    for c in range(chunks):
        intersection = total_grad[c, rows_of(strip), :]
        for peer in strip_peers:
            grad_copy(c, peer, peer).wait_recv()
            intersection = intersection + grad_in[c, peer].astype(jnp.float32)
        projection = total_rays[c, rows_of(strip), :]
        for peer in strip_peers:
            dense_copy(c, peer, peer).wait_recv()
            projection = projection + dense_in[c, peer].astype(jnp.float32)
        part = pl.ds(c, columns, stride=chunks)
        part_field, part_dual = field[part, :], dual[part, :]
        updated = part_field - object_step * (
            intersection + part_dual + penalty * (part_field - projection)
        )
        residual = penalty * (projection - updated) - part_dual
        rows_half[c, rows_of(strip), :] = residual.astype(jnp.bfloat16)
        for peer in strip_peers:
            start(residual_copy(c, strip, peer))
        object_next[part, :] = updated
        dual_next[part, :] = part_dual + penalty * (updated - projection)
    for c in range(chunks):
        for peer in strip_peers:
            residual_copy(c, peer, peer).wait_recv()
        rows = rows_half[c]
        for peer in ang_peers:
            pick_out[c, peer] = dot(picker[peer], rows).astype(jnp.bfloat16)
            start(pick_copy(c, me, peer))
        pick_in[c, me] = dot(picker[me], rows).astype(jnp.bfloat16)
    turned_radon[...] = radon[...].T
    for c in range(chunks):
        for peer in ang_peers:
            pick_copy(c, peer, peer).wait_recv()
        gradient = dot(turned_radon[...], pick_in[c].reshape(angles * hit_rows, slices))
        part = pl.ds(c, pixels, stride=chunks)
        volume_next[part, :] = volume[part, :] - volume_step * gradient
    for copy in started:
        copy.wait_send()


def body(
    measured, positions, probe_field, object_field, dual_field, volume, radon_tiles, tile_range
):
    angles, strips = lax.axis_size("ang"), lax.axis_size("strip")
    frames, side = measured.shape[1], measured.shape[2]
    columns, width = object_field.shape[1], object_field.shape[2] * object_field.shape[3]
    hit_rows = radon_tiles.shape[2] * radon_tiles.shape[3]
    pixels = radon_tiles.shape[4]
    chunks, slices = object_field.shape[2], object_field.shape[3]
    vmem = pl.BlockSpec(memory_space=pltpu.VMEM)
    smem = pl.BlockSpec(memory_space=pltpu.SMEM)
    half = jnp.bfloat16
    outs = pl.pallas_call(
        functools.partial(kernel, angles, strips),
        out_shape=(
            jax.ShapeDtypeStruct((2 * columns, slices), jnp.float32),
            jax.ShapeDtypeStruct((2 * columns, slices), jnp.float32),
            jax.ShapeDtypeStruct((2 * pixels, slices), jnp.float32),
        ),
        in_specs=[smem, smem] + [pl.BlockSpec(memory_space=pltpu.HBM)] * 7,
        out_specs=(vmem, vmem, vmem),
        scratch_shapes=[
            pltpu.VMEM((frames, side, side), jnp.float32),
            pltpu.VMEM((chunks, side, side), jnp.float32),
            pltpu.VMEM((chunks * columns, slices), jnp.float32),
            pltpu.VMEM((chunks * columns, slices), jnp.float32),
            pltpu.VMEM((chunks * pixels, slices), jnp.float32),
            pltpu.VMEM((angles * hit_rows, pixels), half),
            pltpu.VMEM((4, side, side), half),
        ] + [pltpu.VMEM((chunks, angles, hit_rows, slices), half)] * 4 + [
            pltpu.VMEM((columns, width), half),
            pltpu.VMEM((strips, columns, width), half),
        ] + [pltpu.VMEM((chunks, strips, columns, slices), half)] * 4 + [
            pltpu.VMEM((chunks, strips * columns, slices), half),
            pltpu.VMEM((strips * columns, width), jnp.float32),
            pltpu.VMEM((frames * side, width), jnp.float32),
            pltpu.VMEM((chunks, strips * columns, slices), jnp.float32),
            pltpu.VMEM((chunks, strips * columns, slices), jnp.float32),
            pltpu.VMEM((pixels, angles * hit_rows), half),
            pltpu.VMEM((angles, hit_rows, strips * columns), half),
            pltpu.VMEM((strips * columns, angles * hit_rows), half),
            pltpu.SemaphoreType.DMA((7,)),
        ] + [pltpu.SemaphoreType.DMA((chunks, angles))] * 4
        + [pltpu.SemaphoreType.DMA((1 + 3 * chunks, strips))] * 2,
        compiler_params=pltpu.CompilerParams(
            collective_id=0, has_side_effects=True, vmem_limit_bytes=VMEM_BYTES
        ),
    )(
        positions.reshape(frames),
        tile_range.reshape(angles),
        measured[0],
        probe_field,
        object_field.reshape(2 * columns, slices),
        dual_field.reshape(2 * columns, slices),
        volume.reshape(2 * pixels, slices),
        radon_tiles.reshape(angles * hit_rows, pixels),
        jnp.asarray(dft_tables(side)),
    )
    return (
        outs[0].reshape(object_field.shape),
        outs[1].reshape(dual_field.shape),
        outs[2].reshape(volume.shape),
    )


def solution(mesh):
    return jax.shard_map(
        body,
        mesh=mesh,
        in_specs=(
            P("ang", "strip", None, None),
            P("ang", "strip"),
            P(),
            P("ang", "strip", None, None),
            P("ang", "strip", None, None),
            P(("ang", "strip"), None, None),
            P(("ang", "strip"), None, None, None, None),
            P("ang", None, "strip", None),
        ),
        out_specs=(
            P("ang", "strip", None, None),
            P("ang", "strip", None, None),
            P(("ang", "strip"), None, None),
        ),
        check_vma=False,
    )
```
